256 devices in a mesh: layer: 8 (over z_hi, y), feat: 32 (over z_lo, x, core).
Axes of the slice: x: 4, y: 4, z: 8 (z_hi: 2, z_lo: 4; z = z_hi * 4 + z_lo), core: 2. Of those that a mesh axis runs over, the one named last changes fastest.
Arguments:
- residual_in: bfloat16 [8, 1024, 1024], P('layer'), may hold values from -6 to 6
- enc_weight: bfloat16 [8, 1024, 32768], P('layer', None, 'feat'), may hold values from -0.1875 to 0.1875
- enc_bias: float32 [8, 32768], P('layer', 'feat'), may hold values from -3 to 3
- dec_weight: bfloat16 [8, 4, 32768, 1024], P('layer', None, 'feat'), may hold values from -0.03125 to 0.03125
- dec_bias: float32 [8, 1024], P('layer'), may hold values from -3 to 3
Outputs:
- recon: bfloat16 [8, 1024, 1024], P('layer', 'feat')
The draws below stay inside these ranges and needn't reach their ends.
All inputs are finite; a program needn't handle non-finite values.
Results may differ from the reference program's by a relative error of at most 0.023.
Values may be sent and summed in bfloat16 or wider, within the bound.
No kernel may reach another device: no remote copies, remote signals or barrier semaphores. Data moves between devices by JAX's collectives and lax.ppermute only.
A program may use at most 64 MiB of HBM per device.

```python
import jax
import jax.numpy as jnp
from jax import lax

D = 1024
F = 32768
DEPTH = 4
TOK = 1024
LAYERS = 8
N_FEAT = 32


def level_of(own_key, dims, split, least, top_value):
    factor_of, own = 1.0, jax.random.fold_in(own_key, 6)
    for axis_at, blocks in split:
        heights = jnp.exp(jax.random.uniform(jax.random.fold_in(own, axis_at), (blocks,), jnp.float32, least / len(split), top_value / len(split)))
        factor_of = factor_of * jnp.repeat(heights, dims[axis_at] // blocks).reshape([-1 if axis == axis_at else 1 for axis in range(len(dims))])
    return factor_of


def noise(stream_key, dims, deviation, most, shards=(), held_as=jnp.bfloat16):
    gain = level_of(stream_key, dims, shards, -0.22, 0.18) if shards else 1.0
    values = jax.random.normal(stream_key, dims, jnp.float32) * deviation * gain
    return jnp.minimum(jnp.maximum(values, -most), most).astype(held_as)


def setup_inputs(seed: int = 0) -> dict:
    splits = jax.random.split(jax.random.key(seed), 6)
    return {
        "residual_in": noise(splits[0], (LAYERS, TOK, D), 1.0, 6.0, ((0, 8),)),
        "enc_weight": noise(splits[1], (LAYERS, D, F), D ** -0.5, 0.1875, ((0, 8), (2, 32))),
        "enc_bias": noise(splits[2], (LAYERS, F), 0.5, 3.0, ((0, 8), (1, 32)), jnp.float32),
        "dec_weight": noise(splits[3], (LAYERS, DEPTH, F, D), F ** -0.5, 0.03125, ((0, 8), (2, 32))),
        "dec_bias": noise(splits[4], (LAYERS, D), 0.5, 3.0, ((0, 8),), jnp.float32),
    }


def reference(residual_in, enc_weight, enc_bias, dec_weight, dec_bias):
    layers = residual_in.shape[0]
    group_width = F // N_FEAT
    totals = [jnp.zeros((TOK, D), jnp.float32) for target in range(layers)]
    for source in range(layers):
        pre = jnp.dot(residual_in[source], enc_weight[source], preferred_element_type=jnp.float32) + enc_bias[source]
        features = jnp.maximum(pre, 0.0).astype(jnp.bfloat16)
        grouped = features.astype(jnp.float32).reshape(TOK, N_FEAT, group_width)
        for offset in range(DEPTH):
            target = source + offset
            if target < layers:
                weight_now = dec_weight[source, offset].astype(jnp.float32).reshape(N_FEAT, group_width, D)
                partial_value = jnp.einsum("tgf,gfd->gtd", grouped, weight_now)
                rounded = lax.optimization_barrier(partial_value.astype(jnp.bfloat16)).astype(jnp.float32)
                totals[target] = totals[target] + jnp.sum(rounded, axis=0)
    outputs = [(totals[target] + dec_bias[target]).astype(jnp.bfloat16) for target in range(layers)]
    return jnp.stack(outputs, axis=0)
```

```python
import jax
import jax.numpy as jnp
import numpy as np
from jax import lax
from jax.sharding import PartitionSpec as P

DEPTH = 4
Z, X, CORE = 4, 4, 2


def gray(v):
    return v ^ (v >> 1)


def x_flip(core, step):
    return 1 << (core ^ step)


def partner(feat, stage):
    z, x, core = feat // 8, (feat // 2) % 4, feat % 2
    if stage == "core":
        core ^= 1
    elif stage == "x1":
        x = gray(gray(x) ^ x_flip(core, 0))
    elif stage == "x2":
        x = gray(gray(x) ^ x_flip(core, 1))
    elif stage == "z1":
        z ^= 1
    elif stage == "z2":
        z ^= 2
    return z * 8 + x * 2 + core


STAGES = ("core", "x1", "z1", "x2", "z2")


def owners(me):
    z, x, core = me // 8, (me // 2) % 4, me % 2
    p = jnp.arange(32, dtype=jnp.int32)
    o_core = core ^ ((p >> 4) & 1)
    first, second = (p >> 3) & 1, (p >> 1) & 1
    flips = jnp.where(o_core == 0, first | (second << 1), second | (first << 1))
    o_x = gray(gray(x) ^ flips)
    o_z = z ^ (((p >> 2) & 1) | ((p & 1) << 1))
    return o_z * 8 + o_x * 2 + o_core


def exchange(value, stage):
    return lax.ppermute(value, "feat", [(f, partner(f, stage)) for f in range(Z * X * CORE)])


def from_behind(value, axis, steps):
    count = lax.axis_size(axis)
    return lax.ppermute(value, axis, [(source, source + steps) for source in range(0, count - steps)])


def body(residual_in, enc_weight, enc_bias, dec_weight, dec_bias):
    me = lax.axis_index("feat")
    f32, bf16 = jnp.float32, jnp.bfloat16
    tok = residual_in.shape[1]
    rows = residual_in[0].reshape(32, tok // 32, -1)[owners(me)].reshape(tok, -1)
    pre = jnp.dot(rows, enc_weight[0], preferred_element_type=f32) + enc_bias[0]
    features = jnp.maximum(pre, 0.0).astype(bf16)
    total = None
    for offset in (3, 2, 1, 0):
        w = dec_weight[0, offset]
        half = tok // 2
        sent = jnp.dot(features[half:], w, preferred_element_type=f32).astype(bf16)
        kept = jnp.dot(features[:half], w, preferred_element_type=f32).astype(bf16)
        parts = [kept, exchange(sent, "core")]
        n = half
        for stage in STAGES[1:]:
            n //= 2
            out = sum(p[n : 2 * n].astype(f32) for p in parts).astype(bf16)
            parts.append(exchange(out, stage))
        shard = sum(p[:n].astype(f32) for p in parts)
        if offset > 0:
            shard = from_behind(shard.astype(bf16), "layer", offset).astype(f32)
        total = shard if total is None else total + shard
    return (total + dec_bias[0]).astype(bf16)[None]


def solution(mesh):
    in_specs = (
        P("layer", None, None),
        P("layer", None, "feat"),
        P("layer", "feat"),
        P("layer", None, "feat", None),
        P("layer", None),
    )
    out_specs = P("layer", "feat", None)
    return jax.shard_map(body, mesh=mesh, in_specs=in_specs, out_specs=out_specs, check_vma=False)
```
